128 devices in a mesh: dp: 4 (over x), ctx: 32 (over y, z, core).
Axes of the slice: x: 4, y: 4, z: 4, core: 2. Of those that a mesh axis runs over, the one named last changes fastest.
Arguments:
- normed_layer_input: bfloat16 [4, 4096, 8192], P('dp', 'ctx'), may hold values from -6 to 6
- frozen_query_rows: bfloat16 [4, 4096, 8192], P('dp', 'ctx'), may hold values from -160 to 160
- projected_keys: bfloat16 [4, 4096, 1024], P('dp', 'ctx'), may hold values from -7 to 7
- projected_values: bfloat16 [4, 4096, 1024], P('dp', 'ctx'), may hold values from -6 to 6
- output_gradient: bfloat16 [4, 4096, 8192], P('dp', 'ctx'), may hold values from -6 to 6
- adapter_down: bfloat16 [8192, 16], replicated, may hold values from -0.0625 to 0.0625
- adapter_up: bfloat16 [16, 8192], replicated, may hold values from -1.5 to 1.5
- langevin_down_noise: float32 [8192, 16], replicated, may hold values from -1.8 to 1.8
- langevin_up_noise: float32 [16, 8192], replicated, may hold values from -0.6 to 0.6
- listed_key_blocks: int32 [64, 32, 12], replicated, may hold values from 0 to 31, as said below
- head_live_slots: int32 [64], replicated, may hold values from 4 to 12, as said below
Outputs:
- attention: bfloat16 [4, 4096, 8192], P('dp', 'ctx')
- step_down: float32 [8192, 16], replicated
- step_up: float32 [16, 8192], replicated
The draws below stay inside these ranges and needn't reach their ends.
Inputs may be any that keep to these rules, and one draw needn't show every extreme that they name: `listed_key_blocks`: slot 0 of block b's list is b, slot 1 is b - 1, slot 2 is b + 1 (modulo 32), slot 3 is block 0, for every head; the other slots are any blocks. `head_live_slots`: each count is a multiple of 4.
All inputs are finite; a program needn't handle non-finite values.
Results may differ from the reference program's by a relative error of at most 0.013.
Values may be sent and summed in bfloat16 or wider, within the bound.
No kernel may reach another device: no remote copies, remote signals or barrier semaphores. Data moves between devices by JAX's collectives and lax.ppermute only.
A program may use at most 128 MiB of HBM per device.

```python
import jax
import jax.numpy as jnp
from jax import lax

MODEL_WIDTH = 8192
HEAD_SIZE = 128
ADAPTER_RANK = 16
G = 8
BLK = 128
NBMAX = 12
QUERY_HEAD_COUNT = 64
KVH = 8
DOCS = 4
SEQ = 4096
NQB = 32


def draw_head_live_slots(key, part):
    order_perm = jax.random.permutation(jax.random.fold_in(key, 11), QUERY_HEAD_COUNT)
    position = jnp.argsort(order_perm)
    levels = 4 * jax.random.randint(jax.random.fold_in(key, 12), (QUERY_HEAD_COUNT,), 1, NBMAX // 4 + 1)
    levels = jnp.where(position == 0, 4, levels)
    levels = jnp.where(position == 1, NBMAX, levels)
    return levels.astype(jnp.int32)


def draw_listed_key_blocks(key, part):
    blocks = jnp.arange(NQB, dtype=jnp.int32)
    fixed_slots = jnp.stack([blocks, (blocks - 1) % NQB, (blocks + 1) % NQB, jnp.zeros_like(blocks)], axis=1)
    fixed_slots = jnp.broadcast_to(fixed_slots[None], (QUERY_HEAD_COUNT, NQB, 4))
    random_slots = jax.random.randint(jax.random.fold_in(key, 31), (QUERY_HEAD_COUNT, NQB, NBMAX - 4), 0, NQB)
    return jnp.concatenate([fixed_slots, random_slots.astype(jnp.int32)], axis=2).astype(jnp.int32)


def key_field(key):
    field_values = jnp.clip(jax.random.normal(jax.random.fold_in(key, 21), (DOCS, SEQ, KVH * HEAD_SIZE), jnp.float32), -6.0, 6.0)
    return field_values


def draw_projected_keys(key, part):
    return key_field(key).astype(jnp.bfloat16)


def draw_frozen_query_rows(key, part):
    base_values = jnp.clip(jax.random.normal(jax.random.fold_in(key, 23), (DOCS, SEQ, QUERY_HEAD_COUNT * HEAD_SIZE), jnp.float32), -6.0, 6.0)
    return base_values.astype(jnp.bfloat16)


def steps_of(own_key, dims, cuts, least, high):
    def one(dim, shards_of):
        heights = jax.random.uniform(jax.random.fold_in(jax.random.fold_in(own_key, 6), dim), (shards_of,), jnp.float32, least / len(cuts), high / len(cuts))
        return jnp.repeat(jnp.exp(heights), dims[dim] // shards_of).reshape((-1,) + (1,) * (len(dims) - dim - 1))

    loudness = one(*cuts[0])
    for cut in cuts[1:]:
        loudness = loudness * one(*cut)
    return loudness


def noise(own_key, shape, deviation, bound, split=(), kind=jnp.bfloat16):
    gain = steps_of(own_key, shape, split, -0.22, 0.18) if split else 1.0
    drawn = jax.random.normal(own_key, shape, jnp.float32) * deviation * gain
    return jnp.minimum(jnp.maximum(drawn, -bound), bound).astype(kind)


def setup_inputs(seed: int = 0) -> dict:
    keys = jax.random.split(jax.random.key(seed), 12)
    normed_layer_input = noise(keys[0], (DOCS, SEQ, MODEL_WIDTH), 1.0, 6.0, ((0, 4), (1, 32)))
    frozen_query_rows = draw_frozen_query_rows(jax.random.fold_in(keys[11], 71), 0)
    projected_keys = draw_projected_keys(jax.random.fold_in(keys[11], 71), 0)
    projected_values = noise(keys[3], (DOCS, SEQ, KVH * HEAD_SIZE), 1.0, 6.0, ((0, 4), (1, 32)))
    output_gradient = noise(keys[4], (DOCS, SEQ, QUERY_HEAD_COUNT * HEAD_SIZE), 1.0, 6.0, ((0, 4), (1, 32)))
    adapter_down = noise(keys[5], (MODEL_WIDTH, ADAPTER_RANK), MODEL_WIDTH ** -0.5, 0.0625)
    adapter_up = noise(keys[6], (ADAPTER_RANK, QUERY_HEAD_COUNT * HEAD_SIZE), ADAPTER_RANK ** -0.5, 1.5)
    langevin_down_noise = noise(keys[7], (MODEL_WIDTH, ADAPTER_RANK), 0.3, 1.8, (), jnp.float32)
    langevin_up_noise = noise(keys[8], (ADAPTER_RANK, QUERY_HEAD_COUNT * HEAD_SIZE), 0.1, 0.6, (), jnp.float32)
    listed_key_blocks = draw_listed_key_blocks(jax.random.fold_in(keys[11], 71), 0)
    head_live_slots = draw_head_live_slots(jax.random.fold_in(keys[11], 71), 0)
    return dict(normed_layer_input=normed_layer_input, frozen_query_rows=frozen_query_rows, projected_keys=projected_keys, projected_values=projected_values, output_gradient=output_gradient, adapter_down=adapter_down, adapter_up=adapter_up, langevin_down_noise=langevin_down_noise, langevin_up_noise=langevin_up_noise, listed_key_blocks=listed_key_blocks, head_live_slots=head_live_slots)


ADAPTER_GAIN = 2.0
MASK_VALUE = -1.0e30


def attend(queries, cotangent, key_rows, value_rows, live_mask):
    scaling = queries.shape[-1] ** -0.5
    scores = jnp.einsum("gqd,gkd->gqk", queries.astype(jnp.float32), key_rows.astype(jnp.float32)) * scaling
    scores = jnp.where(live_mask[:, None, :], scores, MASK_VALUE)
    largest = jnp.max(scores, axis=-1, keepdims=True)
    shifted = jnp.exp(scores - largest)
    weights = shifted / jnp.sum(shifted, axis=-1, keepdims=True)
    weights_low = weights.astype(jnp.bfloat16)
    outputs = jnp.einsum("gqk,gkd->gqd", weights_low.astype(jnp.float32), value_rows.astype(jnp.float32)).astype(jnp.bfloat16)
    weight_grad = jnp.einsum("gqd,gkd->gqk", cotangent.astype(jnp.float32), value_rows.astype(jnp.float32))
    row_inner = jnp.sum(weights * weight_grad, axis=-1, keepdims=True)
    score_grad = (weights * (weight_grad - row_inner)).astype(jnp.bfloat16)
    query_gradient = (jnp.einsum("gqk,gkd->gqd", score_grad.astype(jnp.float32), key_rows.astype(jnp.float32)) * scaling).astype(jnp.bfloat16)
    return outputs, query_gradient


def block_pass(query_blocks, grad_blocks, key_blocks, value_blocks, slot_lists, live_mask, per_step):
    block_total = query_blocks.shape[0]
    slot_count = slot_lists.shape[1]

    def grouped(tensor):
        return tensor.reshape((block_total // per_step, per_step) + tensor.shape[1:])

    def step_fn(pieces):
        query_part, grad_part, list_part, mask_part = pieces
        key_rows = key_blocks[list_part].reshape(per_step, slot_count * BLK, HEAD_SIZE)
        value_rows = value_blocks[list_part].reshape(per_step, slot_count * BLK, HEAD_SIZE)
        return attend(query_part, grad_part, key_rows, value_rows, mask_part)

    outputs, grads = lax.map(step_fn, (grouped(query_blocks), grouped(grad_blocks), grouped(slot_lists), grouped(live_mask)))
    return outputs.reshape(query_blocks.shape), grads.reshape(query_blocks.shape)


def one_head(query_head, grad_head, key_head, value_head, slot_lists, live_count):
    block_total = slot_lists.shape[0]
    per_step = min(block_total, max(1, 512 // BLK))
    live_row = (jnp.arange(NBMAX * BLK, dtype=jnp.int32) // BLK) < live_count
    live_mask = jnp.broadcast_to(live_row[None, :], (block_total, NBMAX * BLK))
    outputs, grads = block_pass(query_head.reshape(block_total, BLK, HEAD_SIZE), grad_head.reshape(block_total, BLK, HEAD_SIZE),
                                key_head.reshape(block_total, BLK, HEAD_SIZE), value_head.reshape(block_total, BLK, HEAD_SIZE),
                                slot_lists, live_mask, per_step)
    return outputs.reshape(block_total * BLK, HEAD_SIZE), grads.reshape(block_total * BLK, HEAD_SIZE)


def reference(normed_layer_input, frozen_query_rows, projected_keys, projected_values, output_gradient, adapter_down, adapter_up, langevin_down_noise, langevin_up_noise, listed_key_blocks, head_live_slots):
    live_slots = head_live_slots.astype(jnp.int32)
    group_of = jnp.arange(QUERY_HEAD_COUNT, dtype=jnp.int32) // G
    grad_down = jnp.zeros((MODEL_WIDTH, ADAPTER_RANK), jnp.float32)
    up_gradient = jnp.zeros((ADAPTER_RANK, QUERY_HEAD_COUNT * HEAD_SIZE), jnp.float32)
    outputs_all = []
    for document_text in range(DOCS):
        reduced_rank_rows = jnp.dot(normed_layer_input[document_text], adapter_down, preferred_element_type=jnp.float32).astype(jnp.bfloat16)
        query_matrix = (frozen_query_rows[document_text].astype(jnp.float32) + ADAPTER_GAIN * jnp.dot(reduced_rank_rows, adapter_up, preferred_element_type=jnp.float32)).astype(jnp.bfloat16)
        query_heads = query_matrix.reshape(SEQ, QUERY_HEAD_COUNT, HEAD_SIZE).transpose(1, 0, 2)
        grad_heads = output_gradient[document_text].reshape(SEQ, QUERY_HEAD_COUNT, HEAD_SIZE).transpose(1, 0, 2)
        key_heads = projected_keys[document_text].reshape(SEQ, KVH, HEAD_SIZE).transpose(1, 0, 2)
        value_heads = projected_values[document_text].reshape(SEQ, KVH, HEAD_SIZE).transpose(1, 0, 2)

        def per_head(pieces):
            query_head, grad_head, slot_lists, group_index, live_count = pieces
            return one_head(query_head, grad_head, key_heads[group_index], value_heads[group_index], slot_lists, live_count)

        head_out, head_grad = lax.map(per_head, (query_heads, grad_heads, listed_key_blocks, group_of, live_slots))
        attended = head_out.transpose(1, 0, 2).reshape(SEQ, QUERY_HEAD_COUNT * HEAD_SIZE)
        query_gradient = head_grad.transpose(1, 0, 2).reshape(SEQ, QUERY_HEAD_COUNT * HEAD_SIZE)
        up_gradient = up_gradient + ADAPTER_GAIN * jnp.dot(reduced_rank_rows.T, query_gradient, preferred_element_type=jnp.float32)
        reduced_gradient = (ADAPTER_GAIN * jnp.dot(query_gradient, adapter_up.T, preferred_element_type=jnp.float32)).astype(jnp.bfloat16)
        grad_down = grad_down + jnp.dot(normed_layer_input[document_text].T, reduced_gradient, preferred_element_type=jnp.float32)
        outputs_all.append(attended)
    token_norm = (DOCS * SEQ) ** -0.5
    return jnp.stack(outputs_all), grad_down * token_norm + langevin_down_noise, up_gradient * token_norm + langevin_up_noise
```

```python
import functools
import math

import jax
import jax.numpy as jnp
from jax import lax
from jax.experimental import pallas as pl
from jax.experimental.pallas import tpu as pltpu
from jax.sharding import Mesh, PartitionSpec as P

D = 128
HEADS = 32
NBMAX = 12
GAIN = 2.0
SCALE = D**-0.5
EXP2_SCALE = SCALE * math.log2(math.e)
F32, BF16 = jnp.float32, jnp.bfloat16
NT = (((1,), (1,)), ((), ()))
NN = (((1,), (0,)), ((), ()))
TN = (((0,), (0,)), ((), ()))


def attend(quads, base, lists, g, kv, kvt, w_ref, s_ref, q, cot):
    w_ref[0:D, 0:D] = q
    w_ref[D : 2 * D, D : 2 * D] = cot
    w = w_ref[...]

    def block(i, j):
        return lists[base + 4 * i + j]

    def rows(i):
        return pl.ds(512 * i, 512)

    top = jnp.full((8, D), -jnp.inf, F32)
    for i in range(quads):
        tiles = []
        for j in range(4):
            n = block(i, j)
            tiles.append(kv[g, n // 2, pl.ds(pl.multiple_of((n % 2) * D, D), D), :])
        both = lax.dot_general(jnp.concatenate(tiles, axis=0), w, NT, preferred_element_type=F32)
        s_ref[rows(i), :] = both
        top = jnp.maximum(top, both[:, :D].reshape(64, 8, D).max(0))
    largest = jnp.max(top, axis=0, keepdims=True)
    total = jnp.zeros((8, D), F32)
    inner = jnp.zeros((8, D), F32)
    for i in range(quads):
        e = jnp.exp2((s_ref[rows(i), 0:D] - largest) * EXP2_SCALE)
        s_ref[rows(i), 0:D] = e
        total += e.reshape(64, 8, D).sum(0)
        inner += (e * s_ref[rows(i), D : 2 * D]).reshape(64, 8, D).sum(0)
    inverse = 1.0 / jnp.sum(total, axis=0, keepdims=True)
    inner = jnp.sum(inner, axis=0, keepdims=True) * inverse
    out = jnp.zeros((D, D), F32)
    grad = jnp.zeros((D, D), F32)
    for i in range(quads):
        e = s_ref[rows(i), 0:D]
        ds = e * (s_ref[rows(i), D : 2 * D] - inner)
        x = jnp.concatenate([e.astype(BF16), ds.astype(BF16)], axis=1)
        cols = [kvt[g, :, pl.ds(pl.multiple_of(block(i, j) * D, D), D)] for j in range(4)]
        r = lax.dot_general(jnp.concatenate(cols, axis=1), x, NN, preferred_element_type=F32)
        out += r[D : 2 * D, 0:D]
        grad += r[0:D, D : 2 * D]
    return (out * inverse).T.astype(BF16), (grad * (inverse * SCALE)).T.astype(BF16)


def attention_kernel(n_src, copies, lists, live, off, q_own, g_own, qg_far, *rest):
    srcs = rest[:n_src]
    o_own, o_far, d_own, d_far, kv, kvt, w_ref, s_ref, sem = rest[n_src:]
    step = pl.program_id(0)
    del off

    def copy(g, i):
        src, make_src, lo, size, col = copies[g][i]
        return pltpu.make_async_copy(
            make_src(srcs[src]), kv.at[g, lo : lo + size, :, col : col + D], sem.at[g, i]
        )

    @pl.when(step == 0)
    def _():
        for g in range(2):
            for i in range(len(copies[g])):
                copy(g, i).start()
        w_ref[...] = jnp.zeros_like(w_ref)

    for g in range(2):

        @pl.when(step == 8 * g)
        def _():
            for i in range(len(copies[g])):
                copy(g, i).wait()

            def turn(chip, _):
                kvt[g, :, pl.ds(pl.multiple_of(chip * 256, 256), 256)] = kv[g, chip].T
                return 0

            lax.fori_loop(0, 16, turn, 0)

    g = step // 8
    for quads in (1, 2, 3):

        @pl.when(live[step] == 4 * quads)
        def _():
            go = functools.partial(attend, quads)
            out, grad = go(step * 24, lists, g, kv, kvt, w_ref, s_ref, q_own[...], g_own[...])
            o_own[...] = out
            d_own[...] = grad
            out, grad = go(step * 24 + 12, lists, g, kv, kvt, w_ref, s_ref, qg_far[0], qg_far[1])
            o_far[...] = out
            d_far[...] = grad


def attention(chunk, lists, live, off, q_all, g_all, qg_far, srcs, copies):
    whole = pl.BlockSpec((D, D), lambda h, a, b, off: (0, off[0] + h))
    far = pl.BlockSpec((2, D, D), lambda h, a, b, off: (0, 0, 16 * chunk + h))
    res = pl.BlockSpec((D, D), lambda h, a, b, off: (0, h))
    shape = jax.ShapeDtypeStruct((D, 16 * D), BF16)
    n_copies = max(len(c) for c in copies)
    return pl.pallas_call(
        functools.partial(attention_kernel, len(srcs), copies),
        out_shape=(shape,) * 4,
        grid_spec=pltpu.PrefetchScalarGridSpec(
            num_scalar_prefetch=3,
            grid=(16,),
            in_specs=[whole, whole, far] + [pl.BlockSpec(memory_space=pl.ANY)] * len(srcs),
            out_specs=(res,) * 4,
            scratch_shapes=[
                pltpu.VMEM((2, 16, 256, 2 * D), BF16),
                pltpu.VMEM((2, 2 * D, 4096), BF16),
                pltpu.VMEM((2 * D, 2 * D), BF16),
                pltpu.VMEM((NBMAX * D, 2 * D), F32),
                pltpu.SemaphoreType.DMA((2, n_copies)),
            ],
        ),
        compiler_params=pltpu.CompilerParams(
            dimension_semantics=("arbitrary",), vmem_limit_bytes=40 << 20
        ),
        cost_estimate=pl.CostEstimate(
            flops=32 * 8 * 8 * D * D * D, bytes_accessed=8 << 20, transcendentals=32 * 8 * D * D
        ),
        name=f"attend_{chunk}",
    )(lists, live, off, q_all, g_all, qg_far, *srcs)


def hop(x, axis, by):
    return lax.ppermute(x, axis, [(i, (i + by) % 4) for i in range(4)])


def swap(x):
    return lax.ppermute(x, "core", [(0, 1), (1, 0)])


def ring_gather(own, first, second):
    less, more = hop(own, first, 1), hop(own, first, -1)
    k2, v2 = hop(less[0], first, 1), hop(more[1], first, -1)
    line = jnp.stack([own, less, more, jnp.stack([k2, v2])])
    less, more = hop(line, second, 1), hop(line, second, -1)
    k2, v2 = hop(less[:, 0], second, 1), hop(more[:, 1], second, -1)
    return [line, less, more, k2, v2]


def ring_copies(first_src):
    pick = []
    for s in range(3):
        for k in range(2):
            pick.append((first_src + s, lambda r, k=k: r.at[:, k], 4 * s, 4, k * D))
    for k in range(2):
        pick.append((first_src + 3 + k, lambda r: r, 12, 4, k * D))
    return pick


def in_order(own, others, index):
    have = [own, *others]
    out = []
    for j in range(4):
        back = (index - j) % 4
        pick = have[3]
        for d in range(3):
            pick = jnp.where(back == d, have[d], pick)
        out.append(pick)
    return out


def exchange(x, axis):
    return [hop(x, axis, d) for d in (1, 2, 3)]


def all_sum(x, axis):
    low = x.astype(BF16)
    parts = in_order(low, exchange(low, axis), lax.axis_index(axis))
    return sum(p.astype(F32) for p in parts)


def body(x, frozen, keys, values, cot, down, up, noise_down, noise_up, lists, live):
    x, frozen, keys, values, cot = x[0], frozen[0], keys[0], values[0], cot[0]
    core, y, z = lax.axis_index("core"), lax.axis_index("y"), lax.axis_index("z")
    chip = y * 4 + z
    half = HEADS * D

    kv = jnp.stack([keys, values])
    mine = lax.dynamic_slice_in_dim(kv, core * 512, 512, 2)
    far = swap(lax.dynamic_slice_in_dim(kv, (1 - core) * 512, 512, 2))
    kv = jnp.where(core == 0, jnp.concatenate([mine, far], 1), jnp.concatenate([far, mine], 1))
    kv_heads = [kv[:, :, i * D : (i + 1) * D] for i in range(4)]

    late = lax.all_gather(jnp.stack(kv_heads[2:]), ("y", "z"), axis=0, tiled=False)
    ring_a = ring_gather(kv_heads[0], "z", "y")
    ring_b = ring_gather(kv_heads[1], "y", "z")

    low = jnp.dot(x, down, preferred_element_type=F32).astype(BF16)
    query = (frozen.astype(F32) + GAIN * jnp.dot(low, up, preferred_element_type=F32)).astype(BF16)
    away = (1 - core) * half
    qg_far = swap(
        jnp.stack(
            [
                lax.dynamic_slice_in_dim(query, away, half, 1),
                lax.dynamic_slice_in_dim(cot, away, half, 1),
            ]
        )
    )
    low_far = swap(low)

    mylists = lax.dynamic_slice(lists, (core * HEADS, chip * 2, 0), (HEADS, 2, NBMAX))
    mylists = jnp.where(core == 0, mylists, mylists[:, ::-1])
    mylive = lax.dynamic_slice_in_dim(live, core * HEADS, HEADS, 0)
    place = jnp.array([0, 2, 3, 1], jnp.int32)
    at_y = place[(mylists // 8 - y) % 4]
    at_z = place[(mylists // 2 - z) % 4]
    low_bit = mylists % 2
    spot = jnp.concatenate(
        [
            (at_y * 8 + at_z * 2 + low_bit)[:8],
            (at_z * 8 + at_y * 2 + low_bit)[8:16],
            mylists[16:],
        ]
    )

    def run(chunk, srcs, copies):
        return attention(
            chunk,
            spot[16 * chunk : 16 * chunk + 16].reshape(-1),
            mylive[16 * chunk : 16 * chunk + 16],
            jnp.reshape(core * HEADS + 16 * chunk, (1,)),
            query,
            cot,
            qg_far,
            srcs,
            copies,
        )

    early = run(0, ring_a + ring_b, [ring_copies(0), ring_copies(5)])
    gathered = [
        [(0, lambda r, g=g, k=k: r.at[:, g, k], 0, 16, k * D) for k in range(2)] for g in range(2)
    ]
    last = run(1, [late], gathered)

    own_half = jnp.concatenate([early[0], last[0]], axis=1)
    far_half = jnp.concatenate([swap(early[1]), swap(last[1])], axis=1)
    attended = jnp.where(
        core == 0,
        jnp.concatenate([own_half, far_half], 1),
        jnp.concatenate([far_half, own_half], 1),
    )

    d_own = jnp.concatenate([early[2], last[2]], axis=1)
    d_far = jnp.concatenate([early[3], last[3]], axis=1)
    my_up = lax.dynamic_slice_in_dim(up, core * half, half, 1)
    low_grad_far = swap(lax.dot_general(d_far, my_up, NT, preferred_element_type=F32))
    low_grad = lax.dot_general(d_own, my_up, NT, preferred_element_type=F32) + low_grad_far
    low_grad = (GAIN * low_grad).astype(BF16)
    grad_up = GAIN * (
        lax.dot_general(low, d_own, TN, preferred_element_type=F32)
        + lax.dot_general(low_far, d_far, TN, preferred_element_type=F32)
    )
    grad_down = lax.dot_general(low_grad, x, TN, preferred_element_type=F32)
    down_mine = lax.dynamic_slice_in_dim(grad_down, core * half, half, 1)
    down_away = lax.dynamic_slice_in_dim(grad_down, (1 - core) * half, half, 1)
    down_mine = down_mine + swap(down_away.astype(BF16)).astype(F32)

    total = jnp.concatenate([grad_up, down_mine], axis=0)
    quarter = half // 4
    pieces = [
        lax.dynamic_slice_in_dim(total, ((z + d) % 4) * quarter, quarter, 1) for d in range(4)
    ]
    total = pieces[0] + sum(hop(pieces[d].astype(BF16), "z", d).astype(F32) for d in (1, 2, 3))
    total = all_sum(all_sum(total, "y"), "dp").astype(BF16)
    total = jnp.concatenate(in_order(total, exchange(total, "z"), z), axis=1)
    other = swap(total)
    total = jnp.where(
        core == 0, jnp.concatenate([total, other], 1), jnp.concatenate([other, total], 1)
    ).astype(F32)
    norm = (4 * 32 * x.shape[0]) ** -0.5
    step_up = total[:16] * norm + noise_up
    step_down = (total[16:] * norm).T + noise_down
    return attended[None], step_down, step_up


def solution(mesh):
    fine = Mesh(mesh.devices.reshape(4, 4, 4, 2), ("dp", "y", "z", "core"))
    rows = P("dp", ("y", "z", "core"), None)
    return jax.shard_map(
        body,
        mesh=fine,
        in_specs=(rows,) * 5 + (P(),) * 6,
        out_specs=(rows, P(), P()),
        check_vma=False,
    )
```

```python
import functools
import math

import jax
import jax.numpy as jnp
from jax import lax
from jax.experimental import pallas as pl
from jax.experimental.pallas import tpu as pltpu
from jax.sharding import Mesh, PartitionSpec as P

D = 128
HEADS = 32
NBMAX = 12
GAIN = 2.0
SCALE = D**-0.5
EXP2_SCALE = SCALE * math.log2(math.e)
F32, BF16 = jnp.float32, jnp.bfloat16
NT = (((1,), (1,)), ((), ()))
NN = (((1,), (0,)), ((), ()))
TN = (((0,), (0,)), ((), ()))


def attend(quads, lists, bases, g, kv, kvt, w_ref, s_ref, queries, cots):
    def rows(i, part=0, parts=1):
        return pl.ds((512 * i) + part * (512 // parts), 512 // parts)

    def fold(x, op):
        return op(x.reshape(x.shape[0] // 8, 8, D), axis=0)

    def scores(t, out):
        w_ref[t, 0:D, 0:D] = queries[t]
        w_ref[t, D : 2 * D, D : 2 * D] = cots[t]
        w = w_ref[t]
        top = jnp.full((8, D), -jnp.inf, F32)
        for i in range(quads):
            tiles = []
            for j in range(4):
                n = lists[bases[t] + 4 * i + j]
                tiles.append(kv[g, n // 2, pl.ds(pl.multiple_of((n % 2) * D, D), D), :])
            both = lax.dot_general(
                jnp.concatenate(tiles, axis=0), w, NT, preferred_element_type=F32
            )
            s_ref[t, rows(i), :] = both
            top = jnp.maximum(top, fold(both[:, :D], jnp.max))
            yield
        out.append(jnp.max(top, axis=0, keepdims=True))

    def weights(t, largest, out):
        total = jnp.zeros((8, D), F32)
        inner = jnp.zeros((8, D), F32)
        for i in range(quads):
            for part in range(4):
                r = rows(i, part, 4)
                e = jnp.exp2((s_ref[t, r, 0:D] - largest) * EXP2_SCALE)
                s_ref[t, r, 0:D] = e
                total += fold(e, jnp.sum)
                inner += fold(e * s_ref[t, r, D : 2 * D], jnp.sum)
            yield
        inverse = 1.0 / jnp.sum(total, axis=0, keepdims=True)
        out.append((inverse, jnp.sum(inner, axis=0, keepdims=True) * inverse))

    def products(t, inverse, inner, res):
        out = jnp.zeros((D, D), F32)
        grad = jnp.zeros((D, D), F32)
        for i in range(quads):
            e = s_ref[t, rows(i), 0:D]
            ds = e * (s_ref[t, rows(i), D : 2 * D] - inner)
            x = jnp.concatenate([e.astype(BF16), ds.astype(BF16)], axis=1)
            cols = []
            for j in range(4):
                n = lists[bases[t] + 4 * i + j]
                cols.append(kvt[:, pl.ds(pl.multiple_of(n * D, D), D)])
            r = lax.dot_general(jnp.concatenate(cols, axis=1), x, NN, preferred_element_type=F32)
            out += r[D : 2 * D, 0:D]
            grad += r[0:D, D : 2 * D]
            yield
        res.append(((out * inverse).T.astype(BF16), (grad * (inverse * SCALE)).T.astype(BF16)))

    def together(*stages):
        stages = list(stages)
        while stages:
            stages = [s for s in stages if next(s, stages) is not stages]

    tops, sums, results = ([], []), ([], []), []
    together(scores(0, tops[0]))
    together(weights(0, tops[0][0], sums[0]), scores(1, tops[1]))
    together(products(0, *sums[0][0], results), weights(1, tops[1][0], sums[1]))
    together(products(1, *sums[1][0], results))
    return results


def attention_kernel(n_src, copies, lists, live, off, q_own, g_own, qg_far, *rest):
    srcs = rest[:n_src]
    o_own, o_far, d_own, d_far, kv, kvt, w_ref, s_ref, sem = rest[n_src:]
    step = pl.program_id(0)
    del off

    def copy(g, i):
        src, view, lo, size, col = copies[g][i]
        return pltpu.make_async_copy(
            view(srcs[src]), kv.at[g, lo : lo + size, :, col : col + D], sem.at[g, i]
        )

    @pl.when(step == 0)
    def _():
        for g in range(4):
            for i in range(len(copies[g])):
                copy(g, i).start()
        w_ref[...] = jnp.zeros_like(w_ref)

    for g in range(4):

        @pl.when(step == 8 * g)
        def _():
            for i in range(len(copies[g])):
                copy(g, i).wait()

    g = step // 8

    @pl.when(step % 8 == 0)
    def _():
        def turn(chip, _):
            kvt[:, pl.ds(pl.multiple_of(chip * 256, 256), 256)] = kv[g, chip].T
            return 0

        lax.fori_loop(0, 16, turn, 0)

    for quads in (1, 2, 3):

        @pl.when(live[step] == 4 * quads)
        def _():
            bases = (step * 24, step * 24 + 12)
            first, second = attend(
                quads,
                lists,
                bases,
                g,
                kv,
                kvt,
                w_ref,
                s_ref,
                (q_own[...], qg_far[0]),
                (g_own[...], qg_far[1]),
            )
            o_own[...], d_own[...] = first
            o_far[...], d_far[...] = second


def attention(lists, live, off, q_all, g_all, qg_far, srcs, copies):
    whole = pl.BlockSpec((D, D), lambda h, a, b, off: (0, off[0] + h))
    far = pl.BlockSpec((2, D, D), lambda h, a, b, off: (0, 0, h))
    res = pl.BlockSpec((D, D), lambda h, a, b, off: (0, h))
    shape = jax.ShapeDtypeStruct((D, HEADS * D), BF16)
    n_copies = max(len(c) for c in copies)
    return pl.pallas_call(
        functools.partial(attention_kernel, len(srcs), copies),
        out_shape=(shape,) * 4,
        grid_spec=pltpu.PrefetchScalarGridSpec(
            num_scalar_prefetch=3,
            grid=(HEADS,),
            in_specs=[whole, whole, far] + [pl.BlockSpec(memory_space=pl.ANY)] * len(srcs),
            out_specs=(res,) * 4,
            scratch_shapes=[
                pltpu.VMEM((4, 16, 256, 2 * D), BF16),
                pltpu.VMEM((2 * D, 4096), BF16),
                pltpu.VMEM((2, 2 * D, 2 * D), BF16),
                pltpu.VMEM((2, NBMAX * D, 2 * D), F32),
                pltpu.SemaphoreType.DMA((4, n_copies)),
            ],
        ),
        compiler_params=pltpu.CompilerParams(
            dimension_semantics=("arbitrary",), vmem_limit_bytes=40 << 20
        ),
        cost_estimate=pl.CostEstimate(
            flops=64 * 8 * 8 * D * D * D, bytes_accessed=16 << 20, transcendentals=64 * 8 * D * D
        ),
        name="attend",
    )(lists, live, off, q_all, g_all, qg_far, *srcs)


def hop(x, axis, by):
    return lax.ppermute(x, axis, [(i, (i + by) % 4) for i in range(4)])


def swap(x):
    return lax.ppermute(x, "core", [(0, 1), (1, 0)])


def ring_gather(own, first, second):
    less, more = hop(own, first, 1), hop(own, first, -1)
    k2, v2 = hop(less[0], first, 1), hop(more[1], first, -1)
    line = jnp.stack([own, less, more, jnp.stack([k2, v2])])
    less, more = hop(line, second, 1), hop(line, second, -1)
    k2, v2 = hop(less[:, 0], second, 1), hop(more[:, 1], second, -1)
    return [line, less, more, k2, v2]


def ring_copies(first_src, head):
    pick = []
    for s in range(3):
        for k in range(2):
            pick.append((first_src + s, lambda r, k=k: r.at[:, k, head], 4 * s, 4, k * D))
    for k in range(2):
        pick.append((first_src + 3 + k, lambda r: r.at[:, head], 12, 4, k * D))
    return pick


def in_order(own, others, index):
    have = [own, *others]
    out = []
    for j in range(4):
        back = (index - j) % 4
        pick = have[3]
        for d in range(3):
            pick = jnp.where(back == d, have[d], pick)
        out.append(pick)
    return out


def exchange(x, axis):
    return [hop(x, axis, d) for d in (1, 2, 3)]


def all_sum(x, axis):
    low = x.astype(BF16)
    parts = in_order(low, exchange(low, axis), lax.axis_index(axis))
    return sum(p.astype(F32) for p in parts)


def body(x, frozen, keys, values, cot, down, up, noise_down, noise_up, lists, live):
    x, frozen, keys, values, cot = x[0], frozen[0], keys[0], values[0], cot[0]
    core, y, z = lax.axis_index("core"), lax.axis_index("y"), lax.axis_index("z")
    chip = y * 4 + z
    half = HEADS * D

    kv = jnp.stack([keys, values])
    mine = lax.dynamic_slice_in_dim(kv, core * 512, 512, 2)
    far = swap(lax.dynamic_slice_in_dim(kv, (1 - core) * 512, 512, 2))
    kv = jnp.where(core == 0, jnp.concatenate([mine, far], 1), jnp.concatenate([far, mine], 1))
    kv = kv.reshape(2, 256, 4, D).transpose(0, 2, 1, 3)
    ring_a = ring_gather(kv[:, :2], "z", "y")
    ring_b = ring_gather(kv[:, 2:], "y", "z")

    x, frozen, cot, _, _ = lax.optimization_barrier((x, frozen, cot, ring_a[0], ring_b[0]))

    low = jnp.dot(x, down, preferred_element_type=F32).astype(BF16)
    query = (frozen.astype(F32) + GAIN * jnp.dot(low, up, preferred_element_type=F32)).astype(BF16)
    away = (1 - core) * half
    qg_far = swap(
        jnp.stack(
            [
                lax.dynamic_slice_in_dim(query, away, half, 1),
                lax.dynamic_slice_in_dim(cot, away, half, 1),
            ]
        )
    )
    low_far = swap(low)

    mylists = lax.dynamic_slice(lists, (core * HEADS, chip * 2, 0), (HEADS, 2, NBMAX))
    mylists = jnp.where(core == 0, mylists, mylists[:, ::-1])
    mylive = lax.dynamic_slice_in_dim(live, core * HEADS, HEADS, 0)
    place = jnp.array([0, 2, 3, 1], jnp.int32)
    at_y = place[(mylists // 8 - y) % 4]
    at_z = place[(mylists // 2 - z) % 4]
    low_bit = mylists % 2
    spot = jnp.concatenate(
        [
            (at_y * 8 + at_z * 2 + low_bit)[:16],
            (at_z * 8 + at_y * 2 + low_bit)[16:],
        ]
    )
    own_half, far_half, d_own, d_far = attention(
        spot.reshape(-1),
        mylive,
        jnp.reshape(core * HEADS, (1,)),
        query,
        cot,
        qg_far,
        ring_a + ring_b,
        [ring_copies(0, 0), ring_copies(0, 1), ring_copies(5, 0), ring_copies(5, 1)],
    )

    far_half = swap(far_half)
    attended = jnp.where(
        core == 0,
        jnp.concatenate([own_half, far_half], 1),
        jnp.concatenate([far_half, own_half], 1),
    )

    my_up = lax.dynamic_slice_in_dim(up, core * half, half, 1)
    low_grad_far = swap(lax.dot_general(d_far, my_up, NT, preferred_element_type=F32))
    low_grad = lax.dot_general(d_own, my_up, NT, preferred_element_type=F32) + low_grad_far
    low_grad = (GAIN * low_grad).astype(BF16)
    grad_up = GAIN * (
        lax.dot_general(low, d_own, TN, preferred_element_type=F32)
        + lax.dot_general(low_far, d_far, TN, preferred_element_type=F32)
    )
    grad_down = lax.dot_general(low_grad, x, TN, preferred_element_type=F32)
    down_mine = lax.dynamic_slice_in_dim(grad_down, core * half, half, 1)
    down_away = lax.dynamic_slice_in_dim(grad_down, (1 - core) * half, half, 1)
    down_mine = down_mine + swap(down_away.astype(BF16)).astype(F32)

    total = jnp.concatenate([grad_up, down_mine], axis=0)
    quarter = half // 4
    pieces = [
        lax.dynamic_slice_in_dim(total, ((z + d) % 4) * quarter, quarter, 1) for d in range(4)
    ]
    total = pieces[0] + sum(hop(pieces[d].astype(BF16), "z", d).astype(F32) for d in (1, 2, 3))
    total = all_sum(all_sum(total, "y"), "dp").astype(BF16)
    total = jnp.concatenate(in_order(total, exchange(total, "z"), z), axis=1)
    other = swap(total)
    total = jnp.where(
        core == 0, jnp.concatenate([total, other], 1), jnp.concatenate([other, total], 1)
    ).astype(F32)
    norm = (4 * 32 * x.shape[0]) ** -0.5
    step_up = total[:16] * norm + noise_up
    step_down = (total[16:] * norm).T + noise_down
    return attended[None], step_down, step_up


def solution(mesh):
    fine = Mesh(mesh.devices.reshape(4, 4, 4, 2), ("dp", "y", "z", "core"))
    rows = P("dp", ("y", "z", "core"), None)
    return jax.shard_map(
        body,
        mesh=fine,
        in_specs=(rows,) * 5 + (P(),) * 6,
        out_specs=(rows, P(), P()),
        check_vma=False,
    )
```

```python
import functools
import math

import jax
import jax.numpy as jnp
from jax import lax
from jax.experimental import pallas as pl
from jax.experimental.layout import Layout, with_layout_constraint
from jax.experimental.pallas import tpu as pltpu
from jax.sharding import Mesh, PartitionSpec as P

D = 128
HEADS = 32
NBMAX = 12
GAIN = 2.0
SCALE = D**-0.5
EXP2_SCALE = SCALE * math.log2(math.e)
F32, BF16 = jnp.float32, jnp.bfloat16
NT = (((1,), (1,)), ((), ()))
NN = (((1,), (0,)), ((), ()))
TN = (((0,), (0,)), ((), ()))


def attend(quads, zero, lists, bases, g, kv, kvt, w_ref, s_ref, queries, cots):
    def rows(i, part=0, parts=1):
        return pl.ds((512 * i) + part * (512 // parts), 512 // parts)

    def fold(x, op):
        return op(x.reshape(x.shape[0] // 8, 8, D), axis=0)

    def scores(t, out):
        w_ref[t][0:D, 0:D] = queries[t]
        w_ref[t][D : 2 * D, D : 2 * D] = cots[t]
        w = w_ref[t][...]
        top = jnp.full((8, D), -jnp.inf, F32)
        for i in range(quads):
            tiles = []
            for j in range(4):
                n = lists[bases[t] + 4 * i + j]
                tiles.append(kv[g, n // 2, pl.ds(pl.multiple_of((n % 2) * D, D), D), :])
            both = lax.dot_general(
                jnp.concatenate(tiles, axis=0), w, NT, preferred_element_type=F32
            )
            s_ref[t][rows(i), :] = both
            top = jnp.maximum(top, fold(both[:, :D], jnp.max))
            yield
        out.append(jnp.max(top, axis=0, keepdims=True))

    def later(i, part=0, parts=1):
        start = 512 * i + part * (512 // parts)
        return pl.ds(pl.multiple_of(zero + start, 8), 512 // parts)

    def weights(t, largest, out):
        total = jnp.zeros((8, D), F32)
        inner = jnp.zeros((8, D), F32)
        for i in range(quads):
            for part in range(4):
                r = later(i, part, 4)
                e = jnp.exp2((s_ref[t][r, 0:D] - largest) * EXP2_SCALE)
                s_ref[t][r, 0:D] = e
                total += fold(e, jnp.sum)
                inner += fold(e * s_ref[t][r, D : 2 * D], jnp.sum)
            yield
        inverse = 1.0 / jnp.sum(total, axis=0, keepdims=True)
        out.append((inverse, jnp.sum(inner, axis=0, keepdims=True) * inverse))

    def products(t, inverse, inner, res):
        out = jnp.zeros((D, D), F32)
        grad = jnp.zeros((D, D), F32)
        for i in range(quads):
            e = s_ref[t][later(i), 0:D]
            ds = e * (s_ref[t][later(i), D : 2 * D] - inner)
            x = jnp.concatenate([e.astype(BF16), ds.astype(BF16)], axis=1)
            cols = []
            for j in range(4):
                n = lists[bases[t] + 4 * i + j]
                cols.append(kvt[:, pl.ds(pl.multiple_of(n * D, D), D)])
            r = lax.dot_general(jnp.concatenate(cols, axis=1), x, NN, preferred_element_type=F32)
            out += r[D : 2 * D, 0:D]
            grad += r[0:D, D : 2 * D]
            yield
        res.append(((out * inverse).T.astype(BF16), (grad * (inverse * SCALE)).T.astype(BF16)))

    def together(*stages):
        stages = list(stages)
        while stages:
            stages = [s for s in stages if next(s, stages) is not stages]

    tops, sums, results = ([], []), ([], []), []
    together(scores(0, tops[0]))
    together(weights(0, tops[0][0], sums[0]), scores(1, tops[1]))
    together(products(0, *sums[0][0], results), weights(1, tops[1][0], sums[1]))
    together(products(1, *sums[1][0], results))
    return results


def attention_kernel(n_src, copies, lists, live, off, q_own, g_own, qg_far, *rest):
    srcs = rest[:n_src]
    o_own, o_far, d_own, d_far, kv, kvt, w0, w1, sc0, sc1, sem = rest[n_src:]
    w_ref, s_ref = (w0, w1), (sc0, sc1)
    step = pl.program_id(0)

    def copy(g, i):
        src, view, lo, size, col = copies[g][i]
        return pltpu.make_async_copy(
            view(srcs[src]), kv.at[g, lo : lo + size, :, col : col + D], sem.at[g, i]
        )

    @pl.when(step == 0)
    def _():
        for g in range(4):
            for i in range(len(copies[g])):
                copy(g, i).start()
        for w in w_ref:
            w[...] = jnp.zeros_like(w)

    for g in range(4):

        @pl.when(step == 8 * g)
        def _():
            for i in range(len(copies[g])):
                copy(g, i).wait()

    g = step // 8

    @pl.when(step % 8 == 0)
    def _():
        def turn(chip, _):
            kvt[:, pl.ds(pl.multiple_of(chip * 256, 256), 256)] = kv[g, chip].T
            return 0

        lax.fori_loop(0, 16, turn, 0)

    for quads in (1, 2, 3):

        @pl.when(live[step] == 4 * quads)
        def _():
            bases = (step * 24, step * 24 + 12)
            first, second = attend(
                quads,
                off[1],
                lists,
                bases,
                g,
                kv,
                kvt,
                w_ref,
                s_ref,
                (q_own[...], qg_far[0]),
                (g_own[...], qg_far[1]),
            )
            o_own[...], d_own[...] = first
            o_far[...], d_far[...] = second


def attention(lists, live, off, q_all, g_all, qg_far, srcs, copies):
    whole = pl.BlockSpec((D, D), lambda h, a, b, off: (0, off[0] + h))
    far = pl.BlockSpec((2, D, D), lambda h, a, b, off: (0, 0, h))
    res = pl.BlockSpec((D, D), lambda h, a, b, off: (0, h))
    shape = jax.ShapeDtypeStruct((D, HEADS * D), BF16)
    n_copies = max(len(c) for c in copies)
    return pl.pallas_call(
        functools.partial(attention_kernel, len(srcs), copies),
        out_shape=(shape,) * 4,
        grid_spec=pltpu.PrefetchScalarGridSpec(
            num_scalar_prefetch=3,
            grid=(HEADS,),
            in_specs=[whole, whole, far] + [pl.BlockSpec(memory_space=pl.ANY)] * len(srcs),
            out_specs=(res,) * 4,
            scratch_shapes=[
                pltpu.VMEM((4, 16, 256, 2 * D), BF16),
                pltpu.VMEM((2 * D, 4096), BF16),
                pltpu.VMEM((2 * D, 2 * D), BF16),
                pltpu.VMEM((2 * D, 2 * D), BF16),
                pltpu.VMEM((NBMAX * D, 2 * D), F32),
                pltpu.VMEM((NBMAX * D, 2 * D), F32),
                pltpu.SemaphoreType.DMA((4, n_copies)),
            ],
        ),
        compiler_params=pltpu.CompilerParams(
            dimension_semantics=("arbitrary",), vmem_limit_bytes=40 << 20
        ),
        cost_estimate=pl.CostEstimate(
            flops=64 * 8 * 8 * D * D * D, bytes_accessed=16 << 20, transcendentals=64 * 8 * D * D
        ),
        name="attend",
    )(lists, live, off, q_all, g_all, qg_far, *srcs)


def hop(x, axis, by):
    return lax.ppermute(x, axis, [(i, (i + by) % 4) for i in range(4)])


def swap(x):
    return lax.ppermute(x, "core", [(0, 1), (1, 0)])


def row_major(x):
    return with_layout_constraint(x, Layout(major_to_minor=tuple(range(x.ndim))))


def ring_gather(own, first, second):
    less, more = hop(own, first, 1), hop(own, first, -1)
    keys2, values2 = hop(less[0], first, 1), hop(more[1], first, -1)
    keys = row_major(jnp.stack([own[0], less[0], more[0], keys2]))
    values = row_major(jnp.stack([own[1], less[1], more[1], values2]))
    keys_less = hop(keys, second, 1)
    values_more = hop(values, second, -1)
    keys_more, values_less = hop(keys, second, -1), hop(values, second, 1)
    keys2, values2 = hop(keys_less, second, 1), hop(values_more, second, -1)
    return [keys, keys_less, keys_more, keys2, values, values_less, values_more, values2]


def ring_copies(first_src, head):
    return [
        (first_src + 4 * k + s, lambda r: r.at[:, head], 4 * s, 4, k * D)
        for k in range(2)
        for s in range(4)
    ]


def in_order(own, others, index):
    have = [own, *others]
    out = []
    for j in range(4):
        back = (index - j) % 4
        pick = have[3]
        for d in range(3):
            pick = jnp.where(back == d, have[d], pick)
        out.append(pick)
    return out


def exchange(x, axis):
    return [hop(x, axis, 1), hop(x, axis, 2), hop(x, axis, 3)]


def all_sum(x, axis):
    low = x.astype(BF16)
    parts = in_order(low, exchange(low, axis), lax.axis_index(axis))
    return sum(p.astype(F32) for p in parts)


def device(x, frozen, keys, values, cot, down, up, noise_down, noise_up, lists, live):
    x, frozen, keys, values, cot = x[0], frozen[0], keys[0], values[0], cot[0]
    core, y, z = lax.axis_index("core"), lax.axis_index("y"), lax.axis_index("z")
    chip = y * 4 + z
    half = HEADS * D

    kv = jnp.stack([keys, values])
    mine = lax.dynamic_slice_in_dim(kv, core * 512, 512, 2)
    far = swap(lax.dynamic_slice_in_dim(kv, (1 - core) * 512, 512, 2))
    kv = jnp.where(core == 0, jnp.concatenate([mine, far], 1), jnp.concatenate([far, mine], 1))
    heads = [jnp.stack([kv[:, :, i * D : (i + 1) * D] for i in (j, j + 1)], axis=1) for j in (0, 2)]
    ring_a = ring_gather(heads[0], "z", "y")
    ring_b = ring_gather(heads[1], "y", "z")

    x, frozen, cot, *_ = lax.optimization_barrier(
        (x, frozen, cot, ring_a[0], ring_a[4], ring_b[0], ring_b[4])
    )

    low = jnp.dot(x, down, preferred_element_type=F32).astype(BF16)
    query = (frozen.astype(F32) + GAIN * jnp.dot(low, up, preferred_element_type=F32)).astype(BF16)
    away = (1 - core) * half
    qg_far = swap(
        jnp.stack(
            [
                lax.dynamic_slice_in_dim(query, away, half, 1),
                lax.dynamic_slice_in_dim(cot, away, half, 1),
            ]
        )
    )
    low_far = swap(low)

    mylists = lax.dynamic_slice(lists, (core * HEADS, chip * 2, 0), (HEADS, 2, NBMAX))
    mylists = jnp.where(core == 0, mylists, mylists[:, ::-1])
    mylive = lax.dynamic_slice_in_dim(live, core * HEADS, HEADS, 0)
    place = jnp.array([0, 2, 3, 1], jnp.int32)
    at_y = place[(mylists // 8 - y) % 4]
    at_z = place[(mylists // 2 - z) % 4]
    low_bit = mylists % 2
    spot = jnp.concatenate(
        [
            (at_y * 8 + at_z * 2 + low_bit)[:16],
            (at_z * 8 + at_y * 2 + low_bit)[16:],
        ]
    )
    own_half, far_half, d_own, d_far = attention(
        spot.reshape(-1),
        mylive,
        jnp.stack([core * HEADS, 0 * core]),
        query,
        cot,
        qg_far,
        ring_a + ring_b,
        [ring_copies(0, 0), ring_copies(0, 1), ring_copies(8, 0), ring_copies(8, 1)],
    )

    far_half = swap(far_half)
    attended = jnp.where(
        core == 0,
        jnp.concatenate([own_half, far_half], 1),
        jnp.concatenate([far_half, own_half], 1),
    )

    my_up = lax.dynamic_slice_in_dim(up, core * half, half, 1)
    low_grad_far = swap(lax.dot_general(d_far, my_up, NT, preferred_element_type=F32))
    low_grad = lax.dot_general(d_own, my_up, NT, preferred_element_type=F32) + low_grad_far
    low_grad = (GAIN * low_grad).astype(BF16)
    grad_up = GAIN * (
        lax.dot_general(low, d_own, TN, preferred_element_type=F32)
        + lax.dot_general(low_far, d_far, TN, preferred_element_type=F32)
    )
    grad_down = lax.dot_general(low_grad, x, TN, preferred_element_type=F32)
    down_mine = lax.dynamic_slice_in_dim(grad_down, core * half, half, 1)
    down_away = lax.dynamic_slice_in_dim(grad_down, (1 - core) * half, half, 1)
    down_mine = down_mine + swap(down_away.astype(BF16)).astype(F32)

    total = jnp.concatenate([grad_up, down_mine], axis=0)
    quarter = half // 4
    pieces = [
        lax.dynamic_slice_in_dim(total, ((z + d) % 4) * quarter, quarter, 1) for d in range(4)
    ]
    total = pieces[0] + sum(hop(pieces[d].astype(BF16), "z", d).astype(F32) for d in (1, 2, 3))
    total = all_sum(all_sum(total, "y"), "dp").astype(BF16)
    total = jnp.concatenate(in_order(total, exchange(total, "z"), z), axis=1)
    other = swap(total)
    total = jnp.where(
        core == 0, jnp.concatenate([total, other], 1), jnp.concatenate([other, total], 1)
    ).astype(F32)
    norm = (4 * 32 * x.shape[0]) ** -0.5
    step_up = total[:16] * norm + noise_up
    step_down = (total[16:] * norm).T + noise_down
    return attended[None], step_down, step_up


def solution(mesh):
    fine = Mesh(mesh.devices.reshape(4, 4, 4, 2), ("dp", "y", "z", "core"))
    rows = P("dp", ("y", "z", "core"), None)
    return jax.shard_map(
        device,
        mesh=fine,
        in_specs=(rows,) * 5 + (P(),) * 6,
        out_specs=(rows, P(), P()),
        check_vma=False,
    )
```

```python
import functools
import math

import jax
import jax.numpy as jnp
from jax import lax
from jax.experimental import pallas as pl
from jax.experimental.layout import Layout, with_layout_constraint
from jax.experimental.pallas import tpu as pltpu
from jax.sharding import Mesh, PartitionSpec as P

D = 128
HEADS = 32
NBMAX = 12
GAIN = 2.0
SCALE = D**-0.5
EXP2_SCALE = SCALE * math.log2(math.e)
F32, BF16 = jnp.float32, jnp.bfloat16
NT = (((1,), (1,)), ((), ()))
NN = (((1,), (0,)), ((), ()))
TN = (((0,), (0,)), ((), ()))


def attend(quads, zero, lists, bases, g, kv, kvt, w_ref, s_ref, queries, cots):
    def rows(i, part=0, parts=1):
        return pl.ds((512 * i) + part * (512 // parts), 512 // parts)

    def fold(x, op):
        return op(x.reshape(x.shape[0] // 8, 8, D), axis=0)

    def scores(t, out):
        w_ref[t][0:D, 0:D] = queries[t]
        w_ref[t][D : 2 * D, D : 2 * D] = cots[t]
        w = w_ref[t][...]
        top = jnp.full((8, D), -jnp.inf, F32)
        for i in range(quads):
            tiles = []
            for j in range(4):
                n = lists[bases[t] + 4 * i + j]
                tiles.append(kv[g, n // 2, pl.ds(pl.multiple_of((n % 2) * D, D), D), :])
            both = lax.dot_general(
                jnp.concatenate(tiles, axis=0), w, NT, preferred_element_type=F32
            )
            s_ref[t][rows(i), :] = both
            top = jnp.maximum(top, fold(both[:, :D], jnp.max))
            yield
        out.append(jnp.max(top, axis=0, keepdims=True))

    def later(i, part=0, parts=1):
        start = 512 * i + part * (512 // parts)
        return pl.ds(pl.multiple_of(zero + start, 8), 512 // parts)

    def weights(t, largest, out):
        total = jnp.zeros((8, D), F32)
        inner = jnp.zeros((8, D), F32)
        for i in range(quads):
            for part in range(4):
                r = later(i, part, 4)
                e = jnp.exp2((s_ref[t][r, 0:D] - largest) * EXP2_SCALE)
                s_ref[t][r, 0:D] = e
                total += fold(e, jnp.sum)
                inner += fold(e * s_ref[t][r, D : 2 * D], jnp.sum)
            yield
        inverse = 1.0 / jnp.sum(total, axis=0, keepdims=True)
        out.append((inverse, jnp.sum(inner, axis=0, keepdims=True) * inverse))

    def products(t, inverse, inner, res):
        out = jnp.zeros((D, D), F32)
        grad = jnp.zeros((D, D), F32)
        for i in range(quads):
            e = s_ref[t][later(i), 0:D]
            ds = e * (s_ref[t][later(i), D : 2 * D] - inner)
            x = jnp.concatenate([e.astype(BF16), ds.astype(BF16)], axis=1)
            cols = []
            for j in range(4):
                n = lists[bases[t] + 4 * i + j]
                cols.append(kvt[:, pl.ds(pl.multiple_of(n * D, D), D)])
            r = lax.dot_general(jnp.concatenate(cols, axis=1), x, NN, preferred_element_type=F32)
            out += r[D : 2 * D, 0:D]
            grad += r[0:D, D : 2 * D]
            yield
        res.append(((out * inverse).T.astype(BF16), (grad * (inverse * SCALE)).T.astype(BF16)))

    def together(*stages):
        stages = list(stages)
        while stages:
            stages = [s for s in stages if next(s, stages) is not stages]

    tops, sums, results = ([], []), ([], []), []
    together(scores(0, tops[0]))
    together(weights(0, tops[0][0], sums[0]), scores(1, tops[1]))
    together(products(0, *sums[0][0], results), weights(1, tops[1][0], sums[1]))
    together(products(1, *sums[1][0], results))
    return results


def attention_kernel(n_src, copies, lists, live, off, q_own, g_own, qg_far, *rest):
    srcs = rest[:n_src]
    o_own, o_far, d_own, d_far, kv, kvt, w0, w1, sc0, sc1, sem = rest[n_src:]
    w_ref, s_ref = (w0, w1), (sc0, sc1)
    step = pl.program_id(0)

    def copy(g, i):
        src, view, lo, size, col = copies[g][i]
        return pltpu.make_async_copy(
            view(srcs[src]), kv.at[g, lo : lo + size, :, col : col + D], sem.at[g, i]
        )

    @pl.when(step == 0)
    def _():
        for g in range(4):
            for i in range(len(copies[g])):
                copy(g, i).start()
        for w in w_ref:
            w[...] = jnp.zeros_like(w)

    for g in range(4):

        @pl.when(step == 8 * g)
        def _():
            for i in range(len(copies[g])):
                copy(g, i).wait()

    g = step // 8

    @pl.when(step % 8 == 0)
    def _():
        def turn(chip, _):
            kvt[:, pl.ds(pl.multiple_of(chip * 256, 256), 256)] = kv[g, chip].T
            return 0

        lax.fori_loop(0, 16, turn, 0)

    for quads in (1, 2, 3):

        @pl.when(live[step] == 4 * quads)
        def _():
            bases = (step * 24, step * 24 + 12)
            first, second = attend(
                quads,
                off[1],
                lists,
                bases,
                g,
                kv,
                kvt,
                w_ref,
                s_ref,
                (q_own[...], qg_far[0]),
                (g_own[...], qg_far[1]),
            )
            o_own[...], d_own[...] = first
            o_far[...], d_far[...] = second


def attention(lists, live, off, q_all, g_all, qg_far, srcs, copies):
    whole = pl.BlockSpec((D, D), lambda h, a, b, off: (0, off[0] + h))
    far = pl.BlockSpec((2, D, D), lambda h, a, b, off: (0, 0, h))
    res = pl.BlockSpec((D, D), lambda h, a, b, off: (0, h))
    shape = jax.ShapeDtypeStruct((D, HEADS * D), BF16)
    both = jax.ShapeDtypeStruct((D, 2 * HEADS * D), BF16)
    n_copies = max(len(c) for c in copies)
    return pl.pallas_call(
        functools.partial(attention_kernel, len(srcs), copies),
        out_shape=(both, shape, shape, shape),
        grid_spec=pltpu.PrefetchScalarGridSpec(
            num_scalar_prefetch=3,
            grid=(HEADS,),
            in_specs=[whole, whole, far] + [pl.BlockSpec(memory_space=pl.ANY)] * len(srcs),
            out_specs=(whole, res, res, res),
            scratch_shapes=[
                pltpu.VMEM((4, 16, 256, 2 * D), BF16),
                pltpu.VMEM((2 * D, 4096), BF16),
                pltpu.VMEM((2 * D, 2 * D), BF16),
                pltpu.VMEM((2 * D, 2 * D), BF16),
                pltpu.VMEM((NBMAX * D, 2 * D), F32),
                pltpu.VMEM((NBMAX * D, 2 * D), F32),
                pltpu.SemaphoreType.DMA((4, n_copies)),
            ],
        ),
        compiler_params=pltpu.CompilerParams(
            dimension_semantics=("arbitrary",), vmem_limit_bytes=40 << 20
        ),
        cost_estimate=pl.CostEstimate(
            flops=64 * 8 * 8 * D * D * D, bytes_accessed=16 << 20, transcendentals=64 * 8 * D * D
        ),
        name="attend",
    )(lists, live, off, q_all, g_all, qg_far, *srcs)


def hop(x, axis, by):
    return lax.ppermute(x, axis, [(i, (i + by) % 4) for i in range(4)])


def swap(x):
    return lax.ppermute(x, "core", [(0, 1), (1, 0)])


def row_major(x):
    return with_layout_constraint(x, Layout(major_to_minor=tuple(range(x.ndim))))


def ring_gather(own, first, second):
    less, more = hop(own, first, 1), hop(own, first, -1)
    keys2, values2 = hop(less[0], first, 1), hop(more[1], first, -1)
    keys = row_major(jnp.stack([own[0], less[0], more[0], keys2]))
    values = row_major(jnp.stack([own[1], less[1], more[1], values2]))
    keys_less, values_more = hop(keys, second, 1), hop(values, second, -1)
    keys_more, values_less = hop(keys, second, -1), hop(values, second, 1)
    keys2, values2 = hop(keys_less, second, 1), hop(values_more, second, -1)
    return [keys, keys_less, keys_more, keys2, values, values_less, values_more, values2]


def ring_copies(first_src, head):
    return [
        (first_src + 4 * k + s, lambda r: r.at[:, head], 4 * s, 4, k * D)
        for k in range(2)
        for s in range(4)
    ]


def in_order(own, others, index):
    have = [own, *others]
    out = []
    for j in range(4):
        back = (index - j) % 4
        pick = have[3]
        for d in range(3):
            pick = jnp.where(back == d, have[d], pick)
        out.append(pick)
    return out


def exchange(x, axis):
    return [hop(x, axis, 1), hop(x, axis, 2), hop(x, axis, 3)]


def all_sum(x, axis):
    low = x.astype(BF16)
    parts = in_order(low, exchange(low, axis), lax.axis_index(axis))
    return sum(p.astype(F32) for p in parts)


def device(x, frozen, keys, values, cot, down, up, noise_down, noise_up, lists, live):
    x, frozen, keys, values, cot = x[0], frozen[0], keys[0], values[0], cot[0]
    core, y, z = lax.axis_index("core"), lax.axis_index("y"), lax.axis_index("z")
    chip = y * 4 + z
    half = HEADS * D

    kv = jnp.stack([keys, values])
    mine = lax.dynamic_slice_in_dim(kv, core * 512, 512, 2)
    far = swap(lax.dynamic_slice_in_dim(kv, (1 - core) * 512, 512, 2))
    kv = jnp.where(core == 0, jnp.concatenate([mine, far], 1), jnp.concatenate([far, mine], 1))
    heads = [jnp.stack([kv[:, :, i * D : (i + 1) * D] for i in (j, j + 1)], axis=1) for j in (0, 2)]
    ring_a = ring_gather(heads[0], "z", "y")
    ring_b = ring_gather(heads[1], "y", "z")

    x, frozen, cot, *_ = lax.optimization_barrier(
        (x, frozen, cot, ring_a[0], ring_a[4], ring_b[0], ring_b[4])
    )

    low = jnp.dot(x, down, preferred_element_type=F32).astype(BF16)
    query = (frozen.astype(F32) + GAIN * jnp.dot(low, up, preferred_element_type=F32)).astype(BF16)
    away = (1 - core) * half
    qg_far = swap(
        jnp.stack(
            [
                lax.dynamic_slice_in_dim(query, away, half, 1),
                lax.dynamic_slice_in_dim(cot, away, half, 1),
            ]
        )
    )
    low_far = swap(low)

    mylists = lax.dynamic_slice(lists, (core * HEADS, chip * 2, 0), (HEADS, 2, NBMAX))
    mylists = jnp.where(core == 0, mylists, mylists[:, ::-1])
    mylive = lax.dynamic_slice_in_dim(live, core * HEADS, HEADS, 0)
    place = jnp.array([0, 2, 3, 1], jnp.int32)
    at_y = place[(mylists // 8 - y) % 4]
    at_z = place[(mylists // 2 - z) % 4]
    low_bit = mylists % 2
    spot = jnp.concatenate(
        [
            (at_y * 8 + at_z * 2 + low_bit)[:16],
            (at_z * 8 + at_y * 2 + low_bit)[16:],
        ]
    )
    own_half, far_half, d_own, d_far = attention(
        spot.reshape(-1),
        mylive,
        jnp.stack([core * HEADS, 0 * core]),
        query,
        cot,
        qg_far,
        ring_a + ring_b,
        [ring_copies(0, 0), ring_copies(0, 1), ring_copies(8, 0), ring_copies(8, 1)],
    )

    far_half = swap(far_half)
    attended = lax.dynamic_update_slice(own_half, far_half, (0, away))

    my_up = lax.dynamic_slice_in_dim(up, core * half, half, 1)
    low_grad_far = swap(lax.dot_general(d_far, my_up, NT, preferred_element_type=F32))
    low_grad = lax.dot_general(d_own, my_up, NT, preferred_element_type=F32) + low_grad_far
    low_grad = (GAIN * low_grad).astype(BF16)
    grad_up = GAIN * (
        lax.dot_general(low, d_own, TN, preferred_element_type=F32)
        + lax.dot_general(low_far, d_far, TN, preferred_element_type=F32)
    )
    grad_down = lax.dot_general(low_grad, x, TN, preferred_element_type=F32)
    down_mine = lax.dynamic_slice_in_dim(grad_down, core * half, half, 1)
    down_away = lax.dynamic_slice_in_dim(grad_down, (1 - core) * half, half, 1)
    down_mine = down_mine + swap(down_away.astype(BF16)).astype(F32)

    total = jnp.concatenate([grad_up, down_mine], axis=0)
    quarter = half // 4
    pieces = [
        lax.dynamic_slice_in_dim(total, ((z + d) % 4) * quarter, quarter, 1) for d in range(4)
    ]
    total = pieces[0] + sum(hop(pieces[d].astype(BF16), "z", d).astype(F32) for d in (1, 2, 3))
    total = all_sum(all_sum(total, "y"), "dp").astype(BF16)
    total = jnp.concatenate(in_order(total, exchange(total, "z"), z), axis=1)
    other = swap(total)
    total = jnp.where(
        core == 0, jnp.concatenate([total, other], 1), jnp.concatenate([other, total], 1)
    ).astype(F32)
    norm = (4 * 32 * x.shape[0]) ** -0.5
    step_up = total[:16] * norm + noise_up
    step_down = (total[16:] * norm).T + noise_down
    return attended[None], step_down, step_up


def solution(mesh):
    fine = Mesh(mesh.devices.reshape(4, 4, 4, 2), ("dp", "y", "z", "core"))
    rows = P("dp", ("y", "z", "core"), None)
    return jax.shard_map(
        device,
        mesh=fine,
        in_specs=(rows,) * 5 + (P(),) * 6,
        out_specs=(rows, P(), P()),
        check_vma=False,
    )
```

```python
import functools
import math

import jax
import jax.numpy as jnp
from jax import lax
from jax.experimental import pallas as pl
from jax.experimental.layout import Layout, with_layout_constraint
from jax.experimental.pallas import tpu as pltpu
from jax.sharding import Mesh, PartitionSpec as P

D = 128
HEADS = 32
NBMAX = 12
GAIN = 2.0
SCALE = D**-0.5
EXP2_SCALE = SCALE * math.log2(math.e)
F32, BF16 = jnp.float32, jnp.bfloat16
NT = (((1,), (1,)), ((), ()))
NN = (((1,), (0,)), ((), ()))
TN = (((0,), (0,)), ((), ()))


def attend(quads, zero, lists, bases, g, kv, kvt, w_ref, s_ref, queries, cots):
    def rows(i, part=0, parts=1):
        return pl.ds((512 * i) + part * (512 // parts), 512 // parts)

    def fold(x, op):
        return op(x.reshape(x.shape[0] // 8, 8, D), axis=0)

    def scores(t, out):
        w_ref[t][0:D, 0:D] = queries[t]
        w_ref[t][D : 2 * D, D : 2 * D] = cots[t]
        w = w_ref[t][...]
        top = jnp.full((8, D), -jnp.inf, F32)
        for i in range(quads):
            tiles = []
            for j in range(4):
                n = lists[bases[t] + 4 * i + j]
                tiles.append(kv[g, n // 2, pl.ds(pl.multiple_of((n % 2) * D, D), D), :])
            both = lax.dot_general(
                jnp.concatenate(tiles, axis=0), w, NT, preferred_element_type=F32
            )
            s_ref[t][rows(i), :] = both
            top = jnp.maximum(top, fold(both[:, :D], jnp.max))
            yield
        out.append(jnp.max(top, axis=0, keepdims=True))

    def later(i, part=0, parts=1):
        start = 512 * i + part * (512 // parts)
        return pl.ds(pl.multiple_of(zero + start, 8), 512 // parts)

    def weights(t, largest, out):
        total = jnp.zeros((8, D), F32)
        inner = jnp.zeros((8, D), F32)
        for i in range(quads):
            for part in range(4):
                r = later(i, part, 4)
                e = jnp.exp2((s_ref[t][r, 0:D] - largest) * EXP2_SCALE)
                s_ref[t][r, 0:D] = e
                total += fold(e, jnp.sum)
                inner += fold(e * s_ref[t][r, D : 2 * D], jnp.sum)
            yield
        inverse = 1.0 / jnp.sum(total, axis=0, keepdims=True)
        out.append((inverse, jnp.sum(inner, axis=0, keepdims=True) * inverse))

    def products(t, inverse, inner, res):
        out = jnp.zeros((D, D), F32)
        grad = jnp.zeros((D, D), F32)
        for i in range(quads):
            e = s_ref[t][later(i), 0:D]
            ds = e * (s_ref[t][later(i), D : 2 * D] - inner)
            x = jnp.concatenate([e.astype(BF16), ds.astype(BF16)], axis=1)
            cols = []
            for j in range(4):
                n = lists[bases[t] + 4 * i + j]
                cols.append(kvt[:, pl.ds(pl.multiple_of(n * D, D), D)])
            r = lax.dot_general(jnp.concatenate(cols, axis=1), x, NN, preferred_element_type=F32)
            out += r[D : 2 * D, 0:D]
            grad += r[0:D, D : 2 * D]
            yield
        res.append(((out * inverse).T.astype(BF16), (grad * (inverse * SCALE)).T.astype(BF16)))

    def together(*stages):
        stages = list(stages)
        while stages:
            stages = [s for s in stages if next(s, stages) is not stages]

    tops, sums, results = ([], []), ([], []), []
    together(scores(0, tops[0]))
    together(weights(0, tops[0][0], sums[0]), scores(1, tops[1]))
    together(products(0, *sums[0][0], results), weights(1, tops[1][0], sums[1]))
    together(products(1, *sums[1][0], results))
    return results


def attention_kernel(n_src, copies, lists, live, off, q_own, g_own, qg_far, *rest):
    srcs = rest[:n_src]
    o_own, o_far, d_own, d_far, kv, kvt, w0, w1, sc0, sc1, sem = rest[n_src:]
    w_ref, s_ref = (w0, w1), (sc0, sc1)
    step = pl.program_id(0)

    def copy(g, i):
        src, view, lo, size, col = copies[g][i]
        return pltpu.make_async_copy(
            view(srcs[src]), kv.at[g, lo : lo + size, :, col : col + D], sem.at[g, i]
        )

    @pl.when(step == 0)
    def _():
        for g in range(4):
            for i in range(len(copies[g])):
                copy(g, i).start()
        for w in w_ref:
            w[...] = jnp.zeros_like(w)

    for g in range(4):

        @pl.when(step == 8 * g)
        def _():
            for i in range(len(copies[g])):
                copy(g, i).wait()

    g = step // 8

    @pl.when(step % 8 == 0)
    def _():
        def turn(chip, _):
            kvt[:, pl.ds(pl.multiple_of(chip * 256, 256), 256)] = kv[g, chip].T
            return 0

        lax.fori_loop(0, 16, turn, 0)

    for quads in (1, 2, 3):

        @pl.when(live[step] == 4 * quads)
        def _():
            bases = (step * 24, step * 24 + 12)
            first, second = attend(
                quads,
                off[1],
                lists,
                bases,
                g,
                kv,
                kvt,
                w_ref,
                s_ref,
                (q_own[...], qg_far[0]),
                (g_own[...], qg_far[1]),
            )
            o_own[...], d_own[...] = first
            o_far[...], d_far[...] = second


def attention(lists, live, off, q_all, g_all, qg_far, srcs, copies):
    whole = pl.BlockSpec((D, D), lambda h, a, b, off: (0, off[0] + h))
    far = pl.BlockSpec((2, D, D), lambda h, a, b, off: (0, 0, h))
    res = pl.BlockSpec((D, D), lambda h, a, b, off: (0, h))
    shape = jax.ShapeDtypeStruct((D, HEADS * D), BF16)
    both = jax.ShapeDtypeStruct((D, 2 * HEADS * D), BF16)
    n_copies = max(len(c) for c in copies)
    return pl.pallas_call(
        functools.partial(attention_kernel, len(srcs), copies),
        out_shape=(both, shape, shape, shape),
        grid_spec=pltpu.PrefetchScalarGridSpec(
            num_scalar_prefetch=3,
            grid=(HEADS,),
            in_specs=[whole, whole, far] + [pl.BlockSpec(memory_space=pl.ANY)] * len(srcs),
            out_specs=(whole, res, res, res),
            scratch_shapes=[
                pltpu.VMEM((4, 16, 256, 2 * D), BF16),
                pltpu.VMEM((2 * D, 4096), BF16),
                pltpu.VMEM((2 * D, 2 * D), BF16),
                pltpu.VMEM((2 * D, 2 * D), BF16),
                pltpu.VMEM((NBMAX * D, 2 * D), F32),
                pltpu.VMEM((NBMAX * D, 2 * D), F32),
                pltpu.SemaphoreType.DMA((4, n_copies)),
            ],
        ),
        compiler_params=pltpu.CompilerParams(
            dimension_semantics=("arbitrary",), vmem_limit_bytes=42 << 20
        ),
        cost_estimate=pl.CostEstimate(
            flops=64 * 8 * 8 * D * D * D, bytes_accessed=16 << 20, transcendentals=64 * 8 * D * D
        ),
        name="attend",
    )(lists, live, off, q_all, g_all, qg_far, *srcs)


def hop(x, axis, by):
    return lax.ppermute(x, axis, [(i, (i + by) % 4) for i in range(4)])


def swap(x):
    return lax.ppermute(x, "core", [(0, 1), (1, 0)])


def row_major(x):
    return with_layout_constraint(x, Layout(major_to_minor=tuple(range(x.ndim))))


def ring_gather(own, first, second):
    less, more = hop(own, first, 1), hop(own, first, -1)
    keys2, values2 = hop(less[0], first, 1), hop(more[1], first, -1)
    keys = row_major(jnp.stack([own[0], less[0], more[0], keys2]))
    values = row_major(jnp.stack([own[1], less[1], more[1], values2]))
    keys_less, values_more = hop(keys, second, 1), hop(values, second, -1)
    keys_more, values_less = hop(keys, second, -1), hop(values, second, 1)
    keys2, values2 = hop(keys_less, second, 1), hop(values_more, second, -1)
    return [keys, keys_less, keys_more, keys2, values, values_less, values_more, values2]


def ring_copies(first_src, head):
    return [
        (first_src + 4 * k + s, lambda r: r.at[:, head], 4 * s, 4, k * D)
        for k in range(2)
        for s in range(4)
    ]


def in_order(own, others, index):
    have = [own, *others]
    out = []
    for j in range(4):
        back = (index - j) % 4
        pick = have[3]
        for d in range(3):
            pick = jnp.where(back == d, have[d], pick)
        out.append(pick)
    return out


def exchange(x, axis):
    return [hop(x, axis, 1), hop(x, axis, 2), hop(x, axis, 3)]


def all_sum(x, axis):
    low = x.astype(BF16)
    parts = in_order(low, exchange(low, axis), lax.axis_index(axis))
    return sum(p.astype(F32) for p in parts)


def device(x, frozen, keys, values, cot, down, up, noise_down, noise_up, lists, live):
    x, frozen, keys, values, cot = x[0], frozen[0], keys[0], values[0], cot[0]
    core, y, z = lax.axis_index("core"), lax.axis_index("y"), lax.axis_index("z")
    chip = y * 4 + z
    half = HEADS * D

    def half_of(which):
        return jnp.stack(
            [lax.dynamic_slice_in_dim(t, which * 512, 512, 1) for t in (keys, values)]
        )

    mine, far = half_of(core), swap(half_of(1 - core))
    kv = jnp.where(core == 0, jnp.concatenate([mine, far], 1), jnp.concatenate([far, mine], 1))
    heads = [jnp.stack([kv[:, :, i * D : (i + 1) * D] for i in (j, j + 1)], axis=1) for j in (0, 2)]
    ring_a = ring_gather(heads[0], "z", "y")
    ring_b = ring_gather(heads[1], "y", "z")

    x, frozen, cot, *_ = lax.optimization_barrier(
        (x, frozen, cot, ring_a[0], ring_a[4], ring_b[0], ring_b[4])
    )

    low = jnp.dot(x, down, preferred_element_type=F32).astype(BF16)
    query = (frozen.astype(F32) + GAIN * jnp.dot(low, up, preferred_element_type=F32)).astype(BF16)
    away = (1 - core) * half
    qg_far = swap(
        jnp.stack(
            [
                lax.dynamic_slice_in_dim(query, away, half, 1),
                lax.dynamic_slice_in_dim(cot, away, half, 1),
            ]
        )
    )
    low_far = swap(low)

    mylists = lax.dynamic_slice(lists, (core * HEADS, chip * 2, 0), (HEADS, 2, NBMAX))
    mylists = jnp.where(core == 0, mylists, mylists[:, ::-1])
    mylive = lax.dynamic_slice_in_dim(live, core * HEADS, HEADS, 0)
    place = jnp.array([0, 2, 3, 1], jnp.int32)
    at_y = place[(mylists // 8 - y) % 4]
    at_z = place[(mylists // 2 - z) % 4]
    low_bit = mylists % 2
    spot = jnp.concatenate(
        [
            (at_y * 8 + at_z * 2 + low_bit)[:16],
            (at_z * 8 + at_y * 2 + low_bit)[16:],
        ]
    )
    own_half, far_half, d_own, d_far = attention(
        spot.reshape(-1),
        mylive,
        jnp.stack([core * HEADS, 0 * core]),
        query,
        cot,
        qg_far,
        ring_a + ring_b,
        [ring_copies(0, 0), ring_copies(0, 1), ring_copies(8, 0), ring_copies(8, 1)],
    )

    far_half = swap(far_half)
    attended = lax.dynamic_update_slice(own_half, far_half, (0, away))

    my_up = lax.dynamic_slice_in_dim(up, core * half, half, 1)
    low_grad_far = swap(lax.dot_general(d_far, my_up, NT, preferred_element_type=F32))
    low_grad = lax.dot_general(d_own, my_up, NT, preferred_element_type=F32) + low_grad_far
    low_grad = (GAIN * low_grad).astype(BF16)
    grad_up = GAIN * (
        lax.dot_general(low, d_own, TN, preferred_element_type=F32)
        + lax.dot_general(low_far, d_far, TN, preferred_element_type=F32)
    )
    grad_down = lax.dot_general(low_grad, x, TN, preferred_element_type=F32)
    down_mine = lax.dynamic_slice_in_dim(grad_down, core * half, half, 1)
    down_away = lax.dynamic_slice_in_dim(grad_down, (1 - core) * half, half, 1)
    down_mine = down_mine + swap(down_away.astype(BF16)).astype(F32)

    total = jnp.concatenate([grad_up, down_mine], axis=0)
    quarter = half // 4
    pieces = [
        lax.dynamic_slice_in_dim(total, ((z + d) % 4) * quarter, quarter, 1) for d in range(4)
    ]
    total = pieces[0] + sum(hop(pieces[d].astype(BF16), "z", d).astype(F32) for d in (1, 2, 3))
    total = all_sum(all_sum(total, "y"), "dp").astype(BF16)
    total = jnp.concatenate(in_order(total, exchange(total, "z"), z), axis=1)
    other = swap(total)
    total = jnp.where(
        core == 0, jnp.concatenate([total, other], 1), jnp.concatenate([other, total], 1)
    ).astype(F32)
    norm = (4 * 32 * x.shape[0]) ** -0.5
    step_up = total[:16] * norm + noise_up
    step_down = (total[16:] * norm).T + noise_down
    return attended[None], step_down, step_up


def solution(mesh):
    fine = Mesh(mesh.devices.reshape(4, 4, 4, 2), ("dp", "y", "z", "core"))
    rows = P("dp", ("y", "z", "core"), None)
    return jax.shard_map(
        device,
        mesh=fine,
        in_specs=(rows,) * 5 + (P(),) * 6,
        out_specs=(rows, P(), P()),
        check_vma=False,
    )
```
